32 devices in a mesh: row: 4 (over z), col: 8 (over y, x, core).
Axes of the slice: x: 2, y: 2, z: 4, core: 2. Of those that a mesh axis runs over, the one named last changes fastest.
Arguments:
- src_points: bfloat16 [512, 32, 256], P('row'), may hold values from -6 to 6
- tgt_points: bfloat16 [64, 32, 256], P('col'), may hold values from -6 to 6
- log_src: float32 [512, 256], P('row'), may hold values from -4 to 4
- log_tgt: float32 [64, 256], P('col'), may hold values from -4 to 4
- tgt_potential: float32 [64, 256], P('col'), may hold values from -1 to 25
- pattern: int32 [512, 4], P('row'), may hold values from 0 to 63, as said below
Outputs:
- src_new: float32 [512, 256], P('row')
- tgt_new: float32 [64, 256], P('col')
The draws below stay inside these ranges and needn't reach their ends.
Inputs may be any that keep to these rules, and one draw needn't show every extreme that they name: `pattern`: each row names 4 different target blocks. For every index of row and every index of col, at most 128 of the entries in that index's source blocks name a target block held by that index of col, and exactly 128 do for some index of col. Every target block is named by some entry.
All inputs are finite; a program needn't handle non-finite values.
Results may differ from the reference program's by a relative error of at most 0.0015.
Values may be sent and summed in bfloat16 or wider, within the bound.
No kernel may reach another device: no remote copies, remote signals or barrier semaphores. Data moves between devices by JAX's collectives and lax.ppermute only.
A program may use at most 64 MiB of HBM per device.

```python
import jax
import jax.numpy as jnp
from jax import lax

BLK = 256
DIM = 32
FANOUT = 4
TGT_LOCAL = 8
SRC_LOCAL = 128
PAIR_MOST = 128
SRC_BLOCKS = 512
TGT_BLOCKS = 64


def draw_tgt_potential(key, part):
    key_rough = jax.random.fold_in(jax.random.fold_in(key, 11), 0)
    rough = jnp.clip(jax.random.normal(key_rough, (TGT_BLOCKS, BLK), jnp.float32), -3.0, 3.0)
    return 0.3 * rough


def draw_pattern(key, part):
    row_count = SRC_BLOCKS // SRC_LOCAL
    col_count = TGT_BLOCKS // TGT_LOCAL

    def one_shard(shard_key):
        key_swing, key_order, key_offset, key_blocks = jax.random.split(shard_key, 4)
        entry_count = SRC_LOCAL * FANOUT
        remainder = entry_count - PAIR_MOST
        base_count = remainder // (col_count - 1)
        leftover = remainder - base_count * (col_count - 1)
        others = jnp.full((col_count - 1,), base_count, jnp.int32)
        others = others + (jnp.arange(col_count - 1) < leftover).astype(jnp.int32)
        swing = jax.random.randint(key_swing, ((col_count - 2) // 2,), 0, base_count // 4 + 1)
        shifted = jnp.zeros((col_count - 1,), jnp.int32)
        shifted = shifted.at[0:col_count - 2:2].set(swing).at[1:col_count - 2:2].set(-swing)
        others = others + shifted
        ordered = jnp.concatenate([jnp.full((1,), PAIR_MOST, jnp.int32), others])
        shard_order = jax.random.permutation(key_order, col_count)
        counts = jnp.zeros((col_count,), jnp.int32).at[shard_order].set(ordered)
        bounds = jnp.cumsum(counts)
        entries = jnp.arange(entry_count, dtype=jnp.int32)
        owner = jnp.sum((bounds[None, :] <= entries[:, None]).astype(jnp.int32), axis=1)
        offset = jax.random.randint(key_offset, (), 0, TGT_LOCAL)
        target = owner * TGT_LOCAL + (entries + offset) % TGT_LOCAL
        block_order = jax.random.permutation(key_blocks, SRC_LOCAL)
        table = jnp.zeros((SRC_LOCAL, FANOUT), jnp.int32)
        return table.at[block_order[entries // FANOUT], entries % FANOUT].set(target)
    shard_keys = jax.random.split(jax.random.fold_in(key, 7), row_count)
    return jax.vmap(one_shard)(shard_keys).reshape(SRC_BLOCKS, FANOUT)


def block_levels(own_key, dims, cuts, smallest, high):
    level = 1.0
    for dim, shards_of in cuts:
        heights = jax.random.uniform(jax.random.fold_in(jax.random.fold_in(own_key, 6), dim), (shards_of,), jnp.float32, smallest / len(cuts), high / len(cuts))
        level = level * jnp.repeat(jnp.exp(heights), dims[dim] // shards_of).reshape((-1,) + (1,) * (len(dims) - 1 - dim))
    return level


def centred(key, dims, spread, most, cuts=(), held_as=jnp.bfloat16):
    drawn = jax.random.normal(key, dims, jnp.float32) * spread
    if len(cuts) > 0:
        drawn = block_levels(key, dims, cuts, -0.22, 0.18) * drawn
    return jnp.clip(drawn, min=-most, max=most).astype(held_as)


def setup_inputs(seed: int = 0) -> dict:
    key_of = jax.random.split(jax.random.key(seed), 7)
    return {
        "src_points": centred(key_of[0], (SRC_BLOCKS, DIM, BLK), 1.0, 6.0, ((0, 4),)),
        "tgt_points": centred(key_of[1], (TGT_BLOCKS, DIM, BLK), 1.0, 6.0, ((0, 8),)),
        "log_src": centred(key_of[2], (SRC_BLOCKS, BLK), 1.0, 4.0, ((0, 4),), jnp.float32),
        "log_tgt": centred(key_of[3], (TGT_BLOCKS, BLK), 1.0, 4.0, ((0, 8),), jnp.float32),
        "tgt_potential": draw_tgt_potential(jax.random.fold_in(key_of[6], 71), 0),
        "pattern": draw_pattern(jax.random.fold_in(key_of[6], 71), 0),
    }


epsilon = 0.1
very_low = -1e30


def block_costs(src_block, tgt_blocks):
    src_float = src_block.astype(jnp.float32)
    tgt_float = tgt_blocks.astype(jnp.float32)
    products = jnp.einsum("di,kdj->kij", src_float, tgt_float)
    src_square = jnp.sum(src_float * src_float, axis=0)
    tgt_square = jnp.sum(tgt_float * tgt_float, axis=1)
    return (src_square[None, :, None] + tgt_square[:, None, :] - 2.0 * products) / DIM


def reference(src_points, tgt_points, log_src, log_tgt, tgt_potential, pattern):
    def row_block(inputs):
        src_block, targets, log_row = inputs
        costs = block_costs(src_block, tgt_points[targets])
        scores = (tgt_potential[targets][:, None, :] - costs) / epsilon
        top_score = jnp.max(scores, axis=(0, 2))
        exp_total = jnp.sum(jnp.exp(scores - top_score[None, :, None]), axis=(0, 2))
        return epsilon * log_row - epsilon * (top_score + jnp.log(exp_total))

    src_new = lax.map(row_block, (src_points, pattern, log_src))

    def column_block(inputs):
        src_block, targets, src_row = inputs
        costs = block_costs(src_block, tgt_points[targets])
        weights = (src_row[None, :, None] - costs) / epsilon
        top_score = jnp.max(weights, axis=1)
        exp_total = jnp.sum(jnp.exp(weights - top_score[:, None, :]), axis=1)
        return top_score, exp_total

    entry_top, entry_total = lax.map(column_block, (src_points, pattern, src_new))
    flat_ids = pattern.reshape(-1)
    entry_top = entry_top.reshape(-1, BLK)
    entry_total = entry_total.reshape(-1, BLK)
    block_top = jnp.full((TGT_BLOCKS, BLK), very_low, jnp.float32).at[flat_ids].max(entry_top)
    block_total = jnp.zeros((TGT_BLOCKS, BLK), jnp.float32).at[flat_ids].add(
        entry_total * jnp.exp(entry_top - block_top[flat_ids]))
    tgt_new = epsilon * log_tgt - epsilon * (block_top + jnp.log(block_total))
    return (src_new, tgt_new)
```

```python
import math

import jax
import jax.numpy as jnp
from jax import lax
from jax.experimental import pallas as pl
from jax.experimental.pallas import tpu as pltpu
from jax.sharding import PartitionSpec as P

epsilon = 0.1
very_low = -1e30
tiny_sum = 2.0**-100
log2_e = math.log2(math.e)
ln_2 = math.log(2.0)
depth = 128
tail_rows = 16
unroll = 4


def parts3(value):
    high = value.astype(jnp.bfloat16).astype(jnp.float32)
    rest = value - high
    middle = rest.astype(jnp.bfloat16).astype(jnp.float32)
    return high, middle, rest - middle


def lse2(left, right):
    top = jnp.maximum(left, right)
    low = jnp.minimum(left, right)
    return top + jnp.log2(1.0 + jnp.exp2(low - top))


def pad_rows(value, rows):
    return jnp.concatenate(
        [value, jnp.zeros((rows - value.shape[0],) + value.shape[1:], value.dtype)], axis=0
    )


def source_matrix(x_ref, tail_ref, s):
    x = x_ref[s]
    return pad_rows(jnp.concatenate([x, x, tail_ref[s]], axis=0), depth)


def tail_of(value, first):
    high, middle, low = parts3(value)
    row = lax.broadcasted_iota(jnp.int32, (tail_rows, value.shape[-1]), 0)
    ones_at, parts_at = (0, 3) if first else (3, 0)
    out = jnp.where((row >= ones_at) & (row < ones_at + 3), 1.0, 0.0)
    out = jnp.where(row == parts_at, high, out)
    out = jnp.where(row == parts_at + 1, middle, out)
    out = jnp.where(row == parts_at + 2, low, out)
    return out.astype(jnp.bfloat16)


def row_kernel(
    pattern_ref, own_ref, other_ref, own_pot_ref, other_pot_ref, src_ref,
    out_ref, y_ref, list_ref, count_ref,
    x_ref, tail_ref, z_ref, m_ref, s_count, sem,
):
    half, dim, cells = x_ref.shape
    own = own_ref.shape[0]
    pool = 2 * own
    fanout = pattern_ref.shape[1]
    scale = 2.0 * log2_e / (dim * epsilon)
    square_scale = log2_e / (dim * epsilon)
    col = lax.axis_index("col")
    core = lax.rem(col, 2)
    base = (col - core) * own
    flip = core * own
    copy = pltpu.make_async_copy(src_ref.at[pl.ds(core * half, half)], x_ref, sem)
    copy.start()

    def build_target(points_ref, pot_ref, offset):
        def body(t, _):
            y = points_ref[t].astype(jnp.float32)
            bias = pot_ref[pl.ds(t, 1), :] * (log2_e / epsilon) - square_scale * jnp.sum(
                y * y, axis=0, keepdims=True
            )
            scaled = y * scale
            high = scaled.astype(jnp.bfloat16)
            low = (scaled - high.astype(jnp.float32)).astype(jnp.bfloat16)
            stacked = pad_rows(
                jnp.concatenate([high, low, tail_of(bias, False)], axis=0), depth
            )
            y_ref[offset + t] = stacked.T
            return 0
        lax.fori_loop(0, own, body, 0)

    build_target(own_ref, own_pot_ref, 0)
    build_target(other_ref, other_pot_ref, own)
    top = jnp.maximum(jnp.max(own_pot_ref[...]), jnp.max(other_pot_ref[...])) * (
        log2_e / epsilon
    )

    def scan(s, count):
        s_total = jnp.int32(0)
        for k in range(fanout):
            t = pattern_ref[core * half + s, k] - base
            inside = jnp.where((t >= 0) & (t < pool), 1, 0)
            local = jnp.where(t >= own, t - own, t + own)
            local = jnp.where(core == 0, t, local)
            list_ref[count] = (s << 20) | (s << 8) | (local & 255)
            count = count + inside
            s_total = s_total + inside
        s_count[s] = s_total
        return count
    count = lax.fori_loop(0, half, scan, jnp.int32(0))
    for k in range(unroll):
        list_ref[count + k] = jnp.int32(half << 20)
    turns = (count + unroll - 1) // unroll
    count_ref[0] = turns

    copy.wait()

    def build_tail(s, _):
        x = x_ref[s].astype(jnp.float32)
        square = jnp.sum(x * x, axis=0, keepdims=True) * square_scale
        tail_ref[s] = tail_of(-square - top, True)
        z_ref[s] = jnp.zeros(z_ref.shape[1:], jnp.float32)
        return 0
    lax.fori_loop(0, half, build_tail, 0)

    def scores(entry):
        s = (entry >> 8) & 4095
        t = entry & 255
        return entry >> 20, jnp.dot(
            y_ref[t], source_matrix(x_ref, tail_ref, s), preferred_element_type=jnp.float32
        )

    def fast(turn, _):
        for k in range(unroll):
            row, a = scores(list_ref[turn * unroll + k])
            z_ref[row] += jnp.sum(jnp.exp2(a).reshape(cells // 8, 8, cells), axis=0)
        return 0
    lax.fori_loop(0, turns, fast, 0)

    def finish(s, bad):
        total = jnp.sum(z_ref[s], axis=0, keepdims=True)
        used = s_count[s] > 0
        out_ref[pl.ds(s, 1), :] = jnp.where(used, top + jnp.log2(total), very_low)
        return jnp.maximum(bad, jnp.where((total < tiny_sum) & used, 1.0, 0.0))
    bad = lax.fori_loop(0, half, finish, jnp.zeros((1, cells), jnp.float32))

    @pl.when(jnp.max(bad) > 0.0)
    def _():
        z_ref[...] = jnp.zeros_like(z_ref)
        m_ref[...] = jnp.full_like(m_ref, very_low)

        def slow(turn, _):
            row, a = scores(list_ref[turn])
            a = a.reshape(cells // 8, 8, cells)
            before = m_ref[row]
            after = jnp.maximum(before, jnp.max(a, axis=0))
            z_ref[row] = z_ref[row] * jnp.exp2(before - after) + jnp.sum(
                jnp.exp2(a - after[None]), axis=0
            )
            m_ref[row] = after
            return 0
        lax.fori_loop(0, count, slow, 0)

        def finish_slow(s, _):
            best = jnp.max(m_ref[s], axis=0, keepdims=True)
            total = jnp.sum(z_ref[s] * jnp.exp2(m_ref[s] - best), axis=0, keepdims=True)
            used = s_count[s] > 0
            out_ref[pl.ds(s, 1), :] = jnp.where(used, top + best + jnp.log2(total), very_low)
            return 0
        lax.fori_loop(0, half, finish_slow, 0)


def column_kernel(
    list_ref, count_ref, y_ref, l_ref, l2_ref, log_src_ref, src_ref,
    out_ref,
    x_ref, tail_ref, z_ref, m_ref, t_count, sem,
):
    half, dim, cells = x_ref.shape
    pool = y_ref.shape[0]
    square_scale = log2_e / (dim * epsilon)
    core = lax.rem(lax.axis_index("col"), 2)
    copy = pltpu.make_async_copy(src_ref.at[pl.ds(core * half, half)], x_ref, sem)
    copy.start()
    z_ref[...] = jnp.zeros_like(z_ref)
    turns = count_ref[0]
    for t in range(pool):
        t_count[t] = jnp.int32(0)
    copy.wait()

    def build_tail(s, _):
        x = x_ref[s].astype(jnp.float32)
        square = jnp.sum(x * x, axis=0, keepdims=True) * square_scale
        total = lse2(l_ref[pl.ds(s, 1), :], l2_ref[pl.ds(s, 1), :])
        mass = log_src_ref[pl.ds(core * half + s, 1), :] * log2_e
        tail_ref[s] = tail_of(mass - square - total, True)
        return 0
    lax.fori_loop(0, half, build_tail, 0)

    def scores(entry):
        s = (entry >> 8) & 4095
        t = entry & 255
        row = jnp.where((entry >> 20) == half, pool, t)
        return row, jnp.dot(
            y_ref[t], source_matrix(x_ref, tail_ref, s), preferred_element_type=jnp.float32
        )

    def fast(turn, _):
        for k in range(unroll):
            row, a = scores(list_ref[turn * unroll + k])
            e = jnp.exp2(a)
            z_ref[row] += e[:, :128] + e[:, 128:]
            t_count[row] = jnp.int32(1)
        return 0
    lax.fori_loop(0, turns, fast, 0)

    ones = jnp.ones((8, 128), jnp.float32)

    def finish(t, bad):
        total = lax.dot_general(
            ones, z_ref[t], (((1,), (1,)), ((), ())),
            precision=lax.Precision.HIGHEST, preferred_element_type=jnp.float32,
        )[0:1]
        used = t_count[t] > 0
        out_ref[pl.ds(t, 1), :] = jnp.where(used, jnp.log2(total), very_low)
        return jnp.maximum(bad, jnp.where((total < tiny_sum) & used, 1.0, 0.0))
    bad = lax.fori_loop(0, pool, finish, jnp.zeros((1, cells), jnp.float32))

    @pl.when(jnp.max(bad) > 0.0)
    def _():
        z_ref[...] = jnp.zeros_like(z_ref)
        m_ref[...] = jnp.full_like(m_ref, very_low)

        def slow(turn, _):
            row, a = scores(list_ref[turn])
            before = m_ref[row]
            after = jnp.maximum(before, jnp.maximum(a[:, :128], a[:, 128:]))
            z_ref[row] = (
                z_ref[row] * jnp.exp2(before - after)
                + jnp.exp2(a[:, :128] - after)
                + jnp.exp2(a[:, 128:] - after)
            )
            m_ref[row] = after
            return 0
        lax.fori_loop(0, turns * unroll, slow, 0)

        def finish_slow(t, _):
            best = jnp.max(m_ref[t], axis=1, keepdims=True)
            total = jnp.sum(z_ref[t] * jnp.exp2(m_ref[t] - best), axis=1, keepdims=True)
            column = jnp.broadcast_to(best + jnp.log2(total), (cells, 128))
            used = t_count[t] > 0
            out_ref[pl.ds(t, 1), :] = jnp.where(used, column.T[0:1], very_low)
            return 0
        lax.fori_loop(0, pool, finish_slow, 0)


def row_partials(pattern, own, other, own_pot, other_pot, src_points):
    sources, dim, cells = src_points.shape
    half = sources // 2
    pool = 2 * own.shape[0]
    most = half * pattern.shape[1] + unroll
    smem = pl.BlockSpec(memory_space=pltpu.SMEM)
    vmem = pl.BlockSpec(memory_space=pltpu.VMEM)
    return pl.pallas_call(
        row_kernel,
        name="row_half_step",
        out_shape=(
            jax.ShapeDtypeStruct((half, cells), jnp.float32),
            jax.ShapeDtypeStruct((pool, cells, depth), jnp.bfloat16),
            jax.ShapeDtypeStruct((most,), jnp.int32),
            jax.ShapeDtypeStruct((1,), jnp.int32),
        ),
        in_specs=[smem, vmem, vmem, vmem, vmem, pl.BlockSpec(memory_space=pl.ANY)],
        out_specs=(vmem, vmem, smem, smem),
        scratch_shapes=[
            pltpu.VMEM((half, dim, cells), jnp.bfloat16),
            pltpu.VMEM((half, tail_rows, cells), jnp.bfloat16),
            pltpu.VMEM((half + 1, 8, cells), jnp.float32),
            pltpu.VMEM((half + 1, 8, cells), jnp.float32),
            pltpu.SMEM((half,), jnp.int32),
            pltpu.SemaphoreType.DMA,
        ],
    )(pattern, own, other, own_pot, other_pot, src_points)


def column_partials(pair_list, turns, targets, left, right, log_src, src_points):
    sources, dim, cells = src_points.shape
    half = sources // 2
    pool = targets.shape[0]
    smem = pl.BlockSpec(memory_space=pltpu.SMEM)
    vmem = pl.BlockSpec(memory_space=pltpu.VMEM)
    return pl.pallas_call(
        column_kernel,
        name="column_half_step",
        out_shape=jax.ShapeDtypeStruct((pool, cells), jnp.float32),
        in_specs=[smem, smem, vmem, vmem, vmem, vmem, pl.BlockSpec(memory_space=pl.ANY)],
        out_specs=vmem,
        scratch_shapes=[
            pltpu.VMEM((half, dim, cells), jnp.bfloat16),
            pltpu.VMEM((half, tail_rows, cells), jnp.bfloat16),
            pltpu.VMEM((pool + 1, cells, 128), jnp.float32),
            pltpu.VMEM((pool + 1, cells, 128), jnp.float32),
            pltpu.SMEM((pool + 1,), jnp.int32),
            pltpu.SemaphoreType.DMA,
        ],
    )(pair_list, turns, targets, left, right, log_src, src_points)


def solution(mesh):
    rows, cols = mesh.shape["row"], mesh.shape["col"]

    def swap(value, axis, step):
        size = mesh.shape[axis]
        return lax.ppermute(value, axis, [(i, i ^ step) for i in range(size)])

    def on_device(src_points, tgt_points, log_src, log_tgt, tgt_potential, pattern):
        half = src_points.shape[0] // 2
        own = tgt_points.shape[0]
        core = lax.rem(lax.axis_index("col"), 2)
        other_points = swap(tgt_points, "col", 1)
        other_potential = swap(tgt_potential, "col", 1)
        left, targets, pair_list, turns = row_partials(
            pattern, tgt_points, other_points, tgt_potential, other_potential, src_points
        )
        step = 2
        right = jnp.full_like(left, very_low)
        while step < cols:
            left = lse2(left, right) if step > 2 else left
            right = swap(left, "col", step)
            step *= 2
        own_log = lax.dynamic_slice_in_dim(log_src, core * half, half, 0)
        own_new = epsilon * own_log - (epsilon * ln_2) * lse2(left, right)
        other_new = swap(own_new, "col", 1)
        src_new = jnp.concatenate(
            [jnp.where(core == 0, own_new, other_new), jnp.where(core == 0, other_new, own_new)]
        )
        sums = column_partials(pair_list, turns, targets, left, right, log_src, src_points)
        total = lse2(sums[:own], swap(sums[own:], "col", 1))
        step = 1
        while step < rows:
            total = lse2(total, swap(total, "row", step))
            step *= 2
        tgt_new = epsilon * log_tgt - (epsilon * ln_2) * total + tgt_potential
        return (src_new, tgt_new)

    placed = (
        P("row", None, None),
        P("col", None, None),
        P("row", None),
        P("col", None),
        P("col", None),
        P("row", None),
    )
    return jax.shard_map(
        on_device,
        mesh=mesh,
        in_specs=placed,
        out_specs=(P("row", None), P("col", None)),
        check_vma=False,
    )
```

```python
import functools
import math

import jax
import jax.numpy as jnp
from jax import lax
from jax.experimental import pallas as pl
from jax.experimental.pallas import tpu as pltpu
from jax.sharding import PartitionSpec as P

epsilon = 0.1
very_low = -1e30
tiny_sum = 2.0**-100
log2_e = math.log2(math.e)
ln_2 = math.log(2.0)
depth = 128
tail_rows = 16
unroll = 8


def parts3(value):
    high = value.astype(jnp.bfloat16).astype(jnp.float32)
    rest = value - high
    middle = rest.astype(jnp.bfloat16).astype(jnp.float32)
    return high, middle, rest - middle


def merge(parts):
    top = parts[0]
    for part in parts[1:]:
        top = jnp.maximum(top, part)
    total = jnp.exp2(parts[0] - top)
    for part in parts[1:]:
        total = total + jnp.exp2(part - top)
    return top + jnp.log2(total)


def pad_rows(value, rows):
    return jnp.concatenate(
        [value, jnp.zeros((rows - value.shape[0],) + value.shape[1:], value.dtype)], axis=0
    )


def source_matrix(x_ref, s):
    x = x_ref[s]
    row = lax.broadcasted_iota(jnp.int32, (tail_rows, x.shape[1]), 0)
    ones = jnp.where(row < 3, 1.0, 0.0).astype(x.dtype)
    return pad_rows(jnp.concatenate([x, x, ones], axis=0), depth)


def bias_rows(value):
    high, middle, low = parts3(value)
    row = lax.broadcasted_iota(jnp.int32, (tail_rows, value.shape[-1]), 0)
    out = jnp.where(row == 0, high, jnp.where(row == 1, middle, jnp.where(row == 2, low, 0.0)))
    return out.astype(jnp.bfloat16)


def pair_scores(entry, x_ref, y_ref):
    s = (entry >> 8) & 4095
    t = entry & 255
    return s, t, jnp.dot(
        y_ref[t], source_matrix(x_ref, s), preferred_element_type=jnp.float32
    )


def row_kernel(
    pattern_ref, own_ref, other_ref, own_pot_ref, other_pot_ref, src_ref,
    out_ref, square_ref, y_ref, list_ref, count_ref,
    x_ref, shift_ref, z_ref, m_ref, s_count, sem,
):
    half, dim, cells = x_ref.shape
    own = own_ref.shape[0]
    pool = 2 * own
    fanout = pattern_ref.shape[0]
    scale = 2.0 * log2_e / (dim * epsilon)
    square_scale = log2_e / (dim * epsilon)
    col = lax.axis_index("col")
    core = lax.rem(col, 2)
    base = (col - core) * own
    copy = pltpu.make_async_copy(src_ref.at[pl.ds(core * half, half)], x_ref, sem)
    copy.start()

    def scan(s, count):
        s_total = jnp.int32(0)
        for k in range(fanout):
            t = pattern_ref[k, core * half + s] - base
            inside = jnp.where((t >= 0) & (t < pool), 1, 0)
            local = t + core * own
            local = jnp.where(local >= pool, local - pool, local)
            list_ref[count] = (s << 20) | (s << 8) | (local & 255)
            count = count + inside
            s_total = s_total + inside
        s_count[s] = s_total
        return count
    count = lax.fori_loop(0, half, scan, jnp.int32(0), unroll=8)
    for k in range(unroll):
        list_ref[count + k] = jnp.int32(half << 20)
    turns = (count + unroll - 1) // unroll
    count_ref[0] = turns

    def build_target(points_ref, pot_ref, offset):
        def body(t, _):
            y = points_ref[t].astype(jnp.float32)
            bias = pot_ref[pl.ds(t, 1), :] * (log2_e / epsilon) - square_scale * jnp.sum(
                y * y, axis=0, keepdims=True
            )
            scaled = y * scale
            high = scaled.astype(jnp.bfloat16)
            low = (scaled - high.astype(jnp.float32)).astype(jnp.bfloat16)
            stacked = pad_rows(jnp.concatenate([high, low, bias_rows(bias)], axis=0), depth)
            y_ref[offset + t] = stacked.T
            return 0
        lax.fori_loop(0, own, body, 0, unroll=2)

    build_target(own_ref, own_pot_ref, 0)
    build_target(other_ref, other_pot_ref, own)
    top = jnp.maximum(jnp.max(own_pot_ref[...]), jnp.max(other_pot_ref[...])) * (
        log2_e / epsilon
    )
    z_ref[...] = jnp.zeros_like(z_ref)
    copy.wait()

    def build_square(s, _):
        x = x_ref[s].astype(jnp.float32)
        square = jnp.sum(x * x, axis=0, keepdims=True) * square_scale
        square_ref[pl.ds(s, 1), :] = square
        shift_ref[pl.ds(s, 1), :] = -top - square
        return 0
    lax.fori_loop(0, half, build_square, 0, unroll=8)

    def fast(turn, _):
        for k in range(unroll):
            entry = list_ref[turn * unroll + k]
            s, t, a = pair_scores(entry, x_ref, y_ref)
            e = jnp.exp2(a + shift_ref[pl.ds(s, 1), :])
            z_ref[entry >> 20] += jnp.sum(e.reshape(cells // 8, 8, cells), axis=0)
        return 0
    lax.fori_loop(0, turns, fast, 0)

    def finish(s, bad):
        total = jnp.sum(z_ref[s], axis=0, keepdims=True)
        used = s_count[s] > 0
        out_ref[pl.ds(s, 1), :] = jnp.where(used, top + jnp.log2(total), very_low)
        return jnp.maximum(bad, jnp.where((total < tiny_sum) & used, 1.0, 0.0))
    bad = lax.fori_loop(0, half, finish, jnp.zeros((1, cells), jnp.float32), unroll=8)

    @pl.when(jnp.max(bad) > 0.0)
    def _():
        z_ref[...] = jnp.zeros_like(z_ref)
        m_ref[...] = jnp.full_like(m_ref, very_low)

        def slow(turn, _):
            entry = list_ref[turn]
            s, t, a = pair_scores(entry, x_ref, y_ref)
            a = (a + shift_ref[pl.ds(s, 1), :]).reshape(cells // 8, 8, cells)
            row = entry >> 20
            before = m_ref[row]
            after = jnp.maximum(before, jnp.max(a, axis=0))
            z_ref[row] = z_ref[row] * jnp.exp2(before - after) + jnp.sum(
                jnp.exp2(a - after[None]), axis=0
            )
            m_ref[row] = after
            return 0
        lax.fori_loop(0, count, slow, 0)

        def finish_slow(s, _):
            best = jnp.max(m_ref[s], axis=0, keepdims=True)
            total = jnp.sum(z_ref[s] * jnp.exp2(m_ref[s] - best), axis=0, keepdims=True)
            used = s_count[s] > 0
            out_ref[pl.ds(s, 1), :] = jnp.where(used, top + best + jnp.log2(total), very_low)
            return 0
        lax.fori_loop(0, half, finish_slow, 0)


def column_kernel(part_count, *refs):
    list_ref, count_ref, y_ref, square_ref, log_src_ref, src_ref = refs[:6]
    part_refs = refs[6 : 6 + part_count]
    own_ref, other_ref, new_ref = refs[6 + part_count : 9 + part_count]
    x_ref, shift_ref, z_ref, m_ref, t_count, sem = refs[9 + part_count :]
    half, dim, cells = x_ref.shape
    pool = y_ref.shape[0]
    own = pool // 2
    lanes = z_ref.shape[2]
    core = lax.rem(lax.axis_index("col"), 2)
    copy = pltpu.make_async_copy(src_ref.at[pl.ds(core * half, half)], x_ref, sem)
    copy.start()
    z_ref[...] = jnp.zeros_like(z_ref)
    turns = count_ref[0]
    for t in range(pool + 1):
        t_count[t] = jnp.int32(0)
    total = merge([ref[...] for ref in part_refs])
    mass = log_src_ref[pl.ds(pl.multiple_of(core * half, 8), half), :]
    new_ref[...] = epsilon * mass - (epsilon * ln_2) * total
    shift_ref[...] = mass * log2_e - square_ref[...] - total
    copy.wait()

    def scores(entry):
        s, t, a = pair_scores(entry, x_ref, y_ref)
        row = jnp.where((entry >> 20) == half, pool, t)
        return row, a + shift_ref[pl.ds(s, 1), :]

    def fast(turn, _):
        for k in range(unroll):
            row, a = scores(list_ref[turn * unroll + k])
            e = jnp.exp2(a)
            z_ref[row] += e[:, :lanes] + e[:, lanes:]
            t_count[row] = jnp.int32(1)
        return 0
    lax.fori_loop(0, turns, fast, 0)

    ones = jnp.ones((8, lanes), jnp.float32)

    def store(t, value):
        @pl.when(t < own)
        def _():
            own_ref[pl.ds(t, 1), :] = value

        @pl.when(t >= own)
        def _():
            other_ref[pl.ds(t - own, 1), :] = value

    def finish(out_ref, offset):
        bad = jnp.zeros((1, cells), jnp.float32)
        for t in range(own):
            total = lax.dot_general(
                ones, z_ref[offset + t], (((1,), (1,)), ((), ())),
                precision=lax.Precision.HIGHEST, preferred_element_type=jnp.float32,
            )[0:1]
            used = t_count[offset + t] > 0
            out_ref[pl.ds(t, 1), :] = jnp.where(used, jnp.log2(total), very_low)
            bad = jnp.maximum(bad, jnp.where((total < tiny_sum) & used, 1.0, 0.0))
        return bad
    bad = jnp.maximum(finish(other_ref, own), finish(own_ref, 0))

    @pl.when(jnp.max(bad) > 0.0)
    def _():
        z_ref[...] = jnp.zeros_like(z_ref)
        m_ref[...] = jnp.full_like(m_ref, very_low)

        def slow(turn, _):
            row, a = scores(list_ref[turn])
            before = m_ref[row]
            after = jnp.maximum(before, jnp.maximum(a[:, :lanes], a[:, lanes:]))
            z_ref[row] = (
                z_ref[row] * jnp.exp2(before - after)
                + jnp.exp2(a[:, :lanes] - after)
                + jnp.exp2(a[:, lanes:] - after)
            )
            m_ref[row] = after
            return 0
        lax.fori_loop(0, turns * unroll, slow, 0)

        def finish_slow(t, _):
            best = jnp.max(m_ref[t], axis=1, keepdims=True)
            total = jnp.sum(z_ref[t] * jnp.exp2(m_ref[t] - best), axis=1, keepdims=True)
            column = jnp.broadcast_to(best + jnp.log2(total), (cells, lanes))
            used = t_count[t] > 0
            store(t, jnp.where(used, column.T[0:1], very_low))
            return 0
        lax.fori_loop(0, pool, finish_slow, 0)


def vmem_limit(*shapes):
    need = sum(math.prod(shape) * size for shape, size in shapes)
    return need + (8 << 20)


def row_partials(pattern, own, other, own_pot, other_pot, src_points):
    sources, dim, cells = src_points.shape
    half = sources // 2
    pool = 2 * own.shape[0]
    most = half * pattern.shape[0] + unroll
    smem = pl.BlockSpec(memory_space=pltpu.SMEM)
    vmem = pl.BlockSpec(memory_space=pltpu.VMEM)
    return pl.pallas_call(
        row_kernel,
        name="row_half_step",
        out_shape=(
            jax.ShapeDtypeStruct((half, cells), jnp.float32),
            jax.ShapeDtypeStruct((half, cells), jnp.float32),
            jax.ShapeDtypeStruct((pool, cells, depth), jnp.bfloat16),
            jax.ShapeDtypeStruct((most,), jnp.int32),
            jax.ShapeDtypeStruct((1,), jnp.int32),
        ),
        in_specs=[smem, vmem, vmem, vmem, vmem, pl.BlockSpec(memory_space=pl.ANY)],
        out_specs=(vmem, vmem, vmem, smem, smem),
        scratch_shapes=[
            pltpu.VMEM((half, dim, cells), jnp.bfloat16),
            pltpu.VMEM((half, cells), jnp.float32),
            pltpu.VMEM((half + 1, 8, cells), jnp.float32),
            pltpu.VMEM((half + 1, 8, cells), jnp.float32),
            pltpu.SMEM((half,), jnp.int32),
            pltpu.SemaphoreType.DMA,
        ],
        compiler_params=pltpu.CompilerParams(
            vmem_limit_bytes=vmem_limit(
                ((half, dim, cells), 2), ((half + 1, 8, cells), 8), ((half, cells), 12),
                ((pool, cells, depth), 2),
            )
        ),
    )(pattern, own, other, own_pot, other_pot, src_points)


def column_partials(pair_list, turns, targets, squares, log_src, src_points, parts):
    sources, dim, cells = src_points.shape
    half = sources // 2
    pool = targets.shape[0]
    lanes = cells // 2
    smem = pl.BlockSpec(memory_space=pltpu.SMEM)
    vmem = pl.BlockSpec(memory_space=pltpu.VMEM)
    sums = jax.ShapeDtypeStruct((pool // 2, cells), jnp.float32)
    return pl.pallas_call(
        functools.partial(column_kernel, len(parts)),
        name="column_half_step",
        out_shape=(sums, sums, jax.ShapeDtypeStruct((half, cells), jnp.float32)),
        in_specs=[smem, smem, vmem, vmem, vmem, pl.BlockSpec(memory_space=pl.ANY)]
        + [vmem] * len(parts),
        out_specs=(vmem, vmem, vmem),
        scratch_shapes=[
            pltpu.VMEM((half, dim, cells), jnp.bfloat16),
            pltpu.VMEM((half, cells), jnp.float32),
            pltpu.VMEM((pool + 1, cells, lanes), jnp.float32),
            pltpu.VMEM((pool + 1, cells, lanes), jnp.float32),
            pltpu.SMEM((pool + 1,), jnp.int32),
            pltpu.SemaphoreType.DMA,
        ],
        compiler_params=pltpu.CompilerParams(
            vmem_limit_bytes=vmem_limit(
                ((half, dim, cells), 2), ((pool + 1, cells, lanes), 8), ((half, cells), 32),
                ((pool, cells, depth), 2),
            )
        ),
    )(pair_list, turns, targets, squares, log_src, src_points, *parts)


def solution(mesh):
    def swap(value, axis, step):
        size = mesh.shape[axis]
        return lax.ppermute(value, axis, [(i, i ^ step) for i in range(size)])

    def rounds(axis, first):
        size = mesh.shape[axis]
        step = first
        while step < size:
            members = min(4, size // step)
            yield [k * step for k in range(1, members)]
            step *= members

    def on_device(src_points, tgt_points, log_src, log_tgt, tgt_potential, pattern):
        core = lax.rem(lax.axis_index("col"), 2)
        other_points = swap(tgt_points, "col", 1)
        other_potential = swap(tgt_potential, "col", 1)
        left, squares, targets, pair_list, turns = row_partials(
            pattern.T, tgt_points, other_points, tgt_potential, other_potential, src_points
        )
        parts = [left]
        for strides in rounds("col", 2):
            left = merge(parts) if len(parts) > 1 else left
            parts = [left] + [swap(left, "col", stride) for stride in strides]
        own_sums, other_sums, own_new = column_partials(
            pair_list, turns, targets, squares, log_src, src_points, parts
        )
        parts = [own_sums, swap(other_sums, "col", 1)]
        other_new = swap(own_new, "col", 1)
        for strides in rounds("row", 1):
            total = merge(parts)
            parts = [total] + [swap(total, "row", stride) for stride in strides]
        src_new = jnp.concatenate(
            [jnp.where(core == 0, own_new, other_new), jnp.where(core == 0, other_new, own_new)]
        )
        tgt_new = epsilon * log_tgt - (epsilon * ln_2) * merge(parts) + tgt_potential
        return (src_new, tgt_new)

    placed = (
        P("row", None, None),
        P("col", None, None),
        P("row", None),
        P("col", None),
        P("col", None),
        P("row", None),
    )
    return jax.shard_map(
        on_device,
        mesh=mesh,
        in_specs=placed,
        out_specs=(P("row", None), P("col", None)),
        check_vma=False,
    )
```

```python
import functools
import math

import jax
import jax.numpy as jnp
from jax import lax
from jax.experimental import pallas as pl
from jax.experimental.pallas import tpu as pltpu
from jax.sharding import PartitionSpec as P

epsilon = 0.1
very_low = -1e30
tiny_sum = 2.0**-100
log2_e = math.log2(math.e)
ln_2 = math.log(2.0)
depth = 128
tail_rows = 16
unroll = 8


def parts3(value):
    high = value.astype(jnp.bfloat16).astype(jnp.float32)
    rest = value - high
    middle = rest.astype(jnp.bfloat16).astype(jnp.float32)
    return high, middle, rest - middle


def merge(parts):
    top = parts[0]
    for part in parts[1:]:
        top = jnp.maximum(top, part)
    total = jnp.exp2(parts[0] - top)
    for part in parts[1:]:
        total = total + jnp.exp2(part - top)
    return top + jnp.log2(total)


def pad_rows(value, rows):
    return jnp.concatenate(
        [value, jnp.zeros((rows - value.shape[0],) + value.shape[1:], value.dtype)], axis=0
    )


def source_matrix(x_ref, s):
    x = x_ref[s]
    row = lax.broadcasted_iota(jnp.int32, (tail_rows, x.shape[1]), 0)
    ones = jnp.where(row < 3, 1.0, 0.0).astype(x.dtype)
    return pad_rows(jnp.concatenate([x, x, ones], axis=0), depth)


def bias_rows(value):
    high, middle, low = parts3(value)
    row = lax.broadcasted_iota(jnp.int32, (tail_rows, value.shape[-1]), 0)
    out = jnp.where(row == 0, high, jnp.where(row == 1, middle, jnp.where(row == 2, low, 0.0)))
    return out.astype(jnp.bfloat16)


def pair_product(s, t, x_ref, y_ref):
    return jnp.dot(y_ref[t], source_matrix(x_ref, s), preferred_element_type=jnp.float32)


def build_targets(points_ref, pot_ref, y_ref, offset):
    own, dim, cells = points_ref.shape
    scale = 2.0 * log2_e / (dim * epsilon)
    square_scale = log2_e / (dim * epsilon)

    def body(t, _):
        y = points_ref[t].astype(jnp.float32)
        bias = pot_ref[pl.ds(t, 1), :] * (log2_e / epsilon) - square_scale * jnp.sum(
            y * y, axis=0, keepdims=True
        )
        scaled = y * scale
        high = scaled.astype(jnp.bfloat16)
        low = (scaled - high.astype(jnp.float32)).astype(jnp.bfloat16)
        stacked = pad_rows(jnp.concatenate([high, low, bias_rows(bias)], axis=0), depth)
        y_ref[offset + t] = stacked.T
        return 0
    lax.fori_loop(0, own, body, 0, unroll=4)


def prepare_kernel(
    pattern_ref, points_ref, pot_ref, src_ref,
    x_ref, square_ref, y_ref, list_ref, count_ref,
    pattern_scr, code_scr, code_smem, points_scr, pot_scr, sems,
):
    half, dim, cells = x_ref.shape
    own = points_ref.shape[0]
    pool = 2 * own
    fanout, sources = pattern_ref.shape
    square_scale = log2_e / (dim * epsilon)
    col = lax.axis_index("col")
    core = lax.rem(col, 2)
    base = (col - core) * own
    copies = [
        pltpu.make_async_copy(pattern_ref, pattern_scr, sems.at[0]),
        pltpu.make_async_copy(points_ref, points_scr, sems.at[1]),
        pltpu.make_async_copy(pot_ref, pot_scr, sems.at[2]),
        pltpu.make_async_copy(src_ref.at[pl.ds(core * half, half)], x_ref, sems.at[3]),
    ]
    for copy in copies:
        copy.start()

    copies[0].wait()
    t = pattern_scr[...] - base
    inside = (t >= 0) & (t < pool)
    local = t + core * own
    local = jnp.where(local >= pool, local - pool, local)
    s = lax.broadcasted_iota(jnp.int32, (fanout, sources), 1) - core * half
    code_scr[...] = jnp.where(inside, (s << 10) | (local << 1) | 1, 0)
    code_copy = pltpu.make_async_copy(code_scr, code_smem, sems.at[4])
    code_copy.start()

    copies[1].wait()
    copies[2].wait()
    build_targets(points_scr, pot_scr, y_ref, 0)
    copies[3].wait()

    def build_square(s, _):
        x = x_ref[s].astype(jnp.float32)
        square_ref[pl.ds(s, 1), :] = jnp.sum(x * x, axis=0, keepdims=True) * square_scale
        return 0
    lax.fori_loop(0, half, build_square, 0, unroll=8)

    code_copy.wait()

    def scan(s, count):
        for k in range(fanout):
            code = code_smem[k, core * half + s]
            list_ref[count] = code >> 1
            count = count + (code & 1)
        return count
    count = lax.fori_loop(0, half, scan, jnp.int32(0), unroll=8)
    for k in range(unroll):
        list_ref[count + k] = jnp.int32(half << 20)
    count_ref[0] = count


def pair_of(entry):
    return (entry >> 9) & 2047, entry & 511, entry >> 20


def row_kernel(
    list_ref, count_ref, x_ref, square_ref, y_in_ref, other_ref, own_pot_ref, other_pot_ref,
    out_ref, shift_ref, y_ref, e_ref, flag_ref,
    z_ref, m_ref, s_used,
):
    half, dim, cells = x_ref.shape
    own = other_ref.shape[0]
    room = e_ref.shape[0]
    count = count_ref[0]
    turns = (count + unroll - 1) // unroll
    build_targets(other_ref, other_pot_ref, y_ref, own)
    top = jnp.maximum(jnp.max(own_pot_ref[...]), jnp.max(other_pot_ref[...])) * (
        log2_e / epsilon
    )
    z_ref[...] = jnp.zeros_like(z_ref)
    shift_ref[...] = -top - square_ref[...]

    def clear(s, _):
        s_used[s] = jnp.int32(0)
        return 0
    lax.fori_loop(0, half + 1, clear, 0)

    def scores(entry):
        s, t, pad = pair_of(entry)
        a = pair_product(s, t, x_ref, y_ref) + shift_ref[pl.ds(s, 1), :]
        return jnp.where(pad > 0, half, s), a

    def fast(turn, _):
        for k in range(unroll):
            at = turn * unroll + k
            row, a = scores(list_ref[at])
            e = jnp.exp2(a)
            z_ref[row] += jnp.sum(e.reshape(cells // 8, 8, cells), axis=0)
            e_ref[jnp.minimum(at, room - 1)] = e.astype(jnp.bfloat16)
            s_used[row] = jnp.int32(1)
        return 0
    lax.fori_loop(0, turns, fast, 0)

    def finish(s, bad):
        total = jnp.sum(z_ref[s], axis=0, keepdims=True)
        used = s_used[s] > 0
        out_ref[pl.ds(s, 1), :] = jnp.where(used, top + jnp.log2(total), very_low)
        return jnp.maximum(bad, jnp.where((total < tiny_sum) & used, 1.0, 0.0))
    bad = lax.fori_loop(0, half, finish, jnp.zeros((1, cells), jnp.float32), unroll=8)
    redo = (jnp.max(bad) > 0.0) | (count > room)
    flag_ref[0] = jnp.where(redo, 1, 0)

    @pl.when(redo)
    def _():
        z_ref[...] = jnp.zeros_like(z_ref)
        m_ref[...] = jnp.full_like(m_ref, very_low)

        def slow(turn, _):
            row, a = scores(list_ref[turn])
            a = a.reshape(cells // 8, 8, cells)
            before = m_ref[row]
            after = jnp.maximum(before, jnp.max(a, axis=0))
            z_ref[row] = z_ref[row] * jnp.exp2(before - after) + jnp.sum(
                jnp.exp2(a - after[None]), axis=0
            )
            m_ref[row] = after
            return 0
        lax.fori_loop(0, count, slow, 0)

        def finish_slow(s, _):
            best = jnp.max(m_ref[s], axis=0, keepdims=True)
            total = jnp.sum(z_ref[s] * jnp.exp2(m_ref[s] - best), axis=0, keepdims=True)
            used = s_used[s] > 0
            out_ref[pl.ds(s, 1), :] = jnp.where(used, top + best + jnp.log2(total), very_low)
            return 0
        lax.fori_loop(0, half, finish_slow, 0)


def column_kernel(part_count, *refs):
    list_ref, count_ref, flag_ref, x_ref, y_ref, e_ref, square_ref, row_shift_ref = refs[:8]
    log_src_ref = refs[8]
    part_refs = refs[9 : 9 + part_count]
    own_ref, other_ref, new_ref = refs[9 + part_count : 12 + part_count]
    log_scr, weight_ref, shift_ref, acc_ref, z_ref, m_ref, t_used, sem = refs[12 + part_count :]
    half, dim, cells = x_ref.shape
    pool = y_ref.shape[0]
    own = pool // 2
    room = e_ref.shape[0]
    lanes = z_ref.shape[2]
    core = lax.rem(lax.axis_index("col"), 2)
    count = count_ref[0]
    turns = (count + unroll - 1) // unroll
    copy = pltpu.make_async_copy(log_src_ref.at[pl.ds(core * half, half)], log_scr, sem)
    copy.start()
    acc_ref[...] = jnp.zeros_like(acc_ref)
    for t in range(pool + 1):
        t_used[t] = jnp.int32(0)
    total = merge([ref[...] for ref in part_refs])
    copy.wait()
    mass = log_scr[...]
    new_ref[...] = epsilon * mass - (epsilon * ln_2) * total
    shift = mass * log2_e - square_ref[...] - total
    shift_ref[...] = shift
    weight = jnp.where(
        part_refs[0][...] > 0.5 * very_low, jnp.exp2(shift - row_shift_ref[...]), 0.0
    )
    weight_ref[...] = weight
    lowest = jnp.max(weight) * tiny_sum

    def row_of(entry):
        s, t, pad = pair_of(entry)
        return s, t, jnp.where(pad > 0, pool, t)

    @pl.when(flag_ref[0] == 0)
    def _():
        row = lax.broadcasted_iota(jnp.int32, (16, cells), 0)

        def fast(turn, _):
            for k in range(unroll):
                at = turn * unroll + k
                s, t, slot = row_of(list_ref[at])
                w = weight_ref[pl.ds(s, 1), :]
                high = w.astype(jnp.bfloat16).astype(jnp.float32)
                w = jnp.where(row == 0, high, jnp.where(row == 1, w - high, 0.0))
                sums = lax.dot_general(
                    w.astype(jnp.bfloat16), e_ref[jnp.minimum(at, room - 1)],
                    (((1,), (1,)), ((), ())), preferred_element_type=jnp.float32,
                )
                acc_ref[slot] += sums[:8]
                t_used[slot] = jnp.int32(1)
            return 0
        lax.fori_loop(0, turns, fast, 0)

    def finish(out_ref, offset):
        bad = jnp.zeros((1, cells), jnp.float32)
        for t in range(own):
            total = jnp.sum(acc_ref[offset + t], axis=0, keepdims=True)
            used = t_used[offset + t] > 0
            out_ref[pl.ds(t, 1), :] = jnp.where(used, jnp.log2(total), very_low)
            bad = jnp.maximum(bad, jnp.where((total >= lowest) | ~used, 0.0, 1.0))
        return bad
    bad = jnp.maximum(finish(other_ref, own), finish(own_ref, 0))

    @pl.when((jnp.max(bad) > 0.0) | (flag_ref[0] != 0))
    def _():
        z_ref[...] = jnp.zeros_like(z_ref)
        m_ref[...] = jnp.full_like(m_ref, very_low)

        def slow(turn, _):
            s, t, slot = row_of(list_ref[turn])
            a = pair_product(s, t, x_ref, y_ref) + shift_ref[pl.ds(s, 1), :]
            before = m_ref[slot]
            after = jnp.maximum(before, jnp.maximum(a[:, :lanes], a[:, lanes:]))
            z_ref[slot] = (
                z_ref[slot] * jnp.exp2(before - after)
                + jnp.exp2(a[:, :lanes] - after)
                + jnp.exp2(a[:, lanes:] - after)
            )
            m_ref[slot] = after
            t_used[slot] = jnp.int32(1)
            return 0
        lax.fori_loop(0, count, slow, 0)

        def finish_slow(out_ref, offset):
            def body(t, _):
                m = m_ref[offset + t]
                best = jnp.max(m, axis=1, keepdims=True)
                total = jnp.sum(z_ref[offset + t] * jnp.exp2(m - best), axis=1, keepdims=True)
                column = jnp.broadcast_to(best + jnp.log2(total), (cells, lanes))
                used = t_used[offset + t] > 0
                out_ref[pl.ds(t, 1), :] = jnp.where(used, column.T[0:1], very_low)
                return 0
            lax.fori_loop(0, own, body, 0)
        finish_slow(other_ref, own)
        finish_slow(own_ref, 0)


def needs(*shapes):
    return sum(math.prod(shape) * size for shape, size in shapes) + (4 << 20)


hbm = pl.BlockSpec(memory_space=pltpu.HBM)
smem = pl.BlockSpec(memory_space=pltpu.SMEM)
vmem = pl.BlockSpec(memory_space=pltpu.VMEM)


def prepare(pattern, points, potential, src_points):
    sources, dim, cells = src_points.shape
    half = sources // 2
    own = points.shape[0]
    fanout = pattern.shape[0]
    return pl.pallas_call(
        prepare_kernel,
        name="prepare",
        out_shape=(
            jax.ShapeDtypeStruct((half, dim, cells), src_points.dtype),
            jax.ShapeDtypeStruct((half, cells), jnp.float32),
            jax.ShapeDtypeStruct((2 * own, cells, depth), jnp.bfloat16),
            jax.ShapeDtypeStruct((half * fanout + unroll,), jnp.int32),
            jax.ShapeDtypeStruct((1,), jnp.int32),
        ),
        in_specs=[hbm] * 4,
        out_specs=(vmem, vmem, vmem, smem, smem),
        scratch_shapes=[
            pltpu.VMEM(pattern.shape, jnp.int32),
            pltpu.VMEM(pattern.shape, jnp.int32),
            pltpu.SMEM(pattern.shape, jnp.int32),
            pltpu.VMEM(points.shape, points.dtype),
            pltpu.VMEM(potential.shape, potential.dtype),
            pltpu.SemaphoreType.DMA((5,)),
        ],
        cost_estimate=pl.CostEstimate(
            flops=10 * src_points.size, bytes_accessed=2 * src_points.size, transcendentals=0
        ),
        compiler_params=pltpu.CompilerParams(
            vmem_limit_bytes=needs(
                ((half, dim, cells), 2), ((half, cells), 4), ((2 * own, cells, depth), 2),
                (points.shape, 2),
            )
        ),
    )(*[
        pltpu.with_memory_space_constraint(value, pltpu.HBM)
        for value in (pattern, points, potential, src_points)
    ])


def row_partials(pair_list, count, x, squares, targets, other, own_pot, other_pot, room):
    half, dim, cells = x.shape
    return pl.pallas_call(
        row_kernel,
        name="row_half_step",
        out_shape=(
            jax.ShapeDtypeStruct((half, cells), jnp.float32),
            jax.ShapeDtypeStruct((half, cells), jnp.float32),
            jax.ShapeDtypeStruct(targets.shape, targets.dtype),
            pltpu.VMEM((room, cells, cells), jnp.bfloat16),
            jax.ShapeDtypeStruct((1,), jnp.int32),
        ),
        in_specs=[smem, smem, vmem, vmem, vmem, vmem, vmem, vmem],
        out_specs=(vmem, vmem, vmem, vmem, smem),
        input_output_aliases={4: 2},
        scratch_shapes=[
            pltpu.VMEM((half + 1, 8, cells), jnp.float32),
            pltpu.VMEM((half + 1, 8, cells), jnp.float32),
            pltpu.SMEM((half + 1,), jnp.int32),
        ],
        compiler_params=pltpu.CompilerParams(
            vmem_limit_bytes=needs(((half + 1, 8, cells), 8), ((half, cells), 8))
        ),
    )(pair_list, count, x, squares, targets, other, own_pot, other_pot)


def column_partials(pair_list, count, flag, x, targets, kept, squares, shift, log_src, parts):
    half, dim, cells = x.shape
    pool = targets.shape[0]
    lanes = cells // 2
    sums = jax.ShapeDtypeStruct((pool // 2, cells), jnp.float32)
    return pl.pallas_call(
        functools.partial(column_kernel, len(parts)),
        name="column_half_step",
        out_shape=(sums, sums, jax.ShapeDtypeStruct((half, cells), jnp.float32)),
        in_specs=[smem, smem, smem, vmem, vmem, vmem, vmem, vmem, hbm] + [vmem] * len(parts),
        out_specs=(vmem, vmem, vmem),
        scratch_shapes=[
            pltpu.VMEM((half, cells), jnp.float32),
            pltpu.VMEM((half, cells), jnp.float32),
            pltpu.VMEM((half, cells), jnp.float32),
            pltpu.VMEM((pool + 1, 8, cells), jnp.float32),
            pltpu.VMEM((pool + 1, cells, lanes), jnp.float32),
            pltpu.VMEM((pool + 1, cells, lanes), jnp.float32),
            pltpu.SMEM((pool + 1,), jnp.int32),
            pltpu.SemaphoreType.DMA,
        ],
        compiler_params=pltpu.CompilerParams(
            vmem_limit_bytes=needs(((pool + 1, cells, lanes), 8), ((half, cells), 12))
        ),
    )(
        pair_list, count, flag, x, targets, pltpu.with_memory_space_constraint(kept, pltpu.VMEM),
        squares, shift, pltpu.with_memory_space_constraint(log_src, pltpu.HBM), *parts
    )


def solution(mesh):
    def swap(value, axis, step):
        size = mesh.shape[axis]
        return lax.ppermute(value, axis, [(i, i ^ step) for i in range(size)])

    def rounds(axis, first):
        size = mesh.shape[axis]
        step = first
        while step < size:
            members = min(4, size // step)
            yield [k * step for k in range(1, members)]
            step *= members

    def on_device(src_points, tgt_points, log_src, log_tgt, tgt_potential, pattern):
        core = lax.rem(lax.axis_index("col"), 2)
        other_points = swap(tgt_points, "col", 1)
        other_potential = swap(tgt_potential, "col", 1)
        x, squares, targets, pair_list, count = prepare(
            pattern.T, tgt_points, tgt_potential, src_points
        )
        chips = mesh.shape["col"] // 2
        entries = x.shape[0] * pattern.shape[1]
        room = min(entries, 3 * -(-entries // (chips * unroll)) * unroll)
        left, shift, targets, kept, flag = row_partials(
            pair_list, count, x, squares, targets, other_points, tgt_potential,
            other_potential, room,
        )
        parts = [left]
        for strides in rounds("col", 2):
            left = merge(parts) if len(parts) > 1 else left
            parts = [left] + [swap(left, "col", stride) for stride in strides]
        own_sums, other_sums, own_new = column_partials(
            pair_list, count, flag, x, targets, kept, squares, shift, log_src, parts
        )
        parts = [own_sums, swap(other_sums, "col", 1)]
        other_new = swap(own_new, "col", 1)
        for strides in rounds("row", 1):
            total = merge(parts)
            parts = [total] + [swap(total, "row", stride) for stride in strides]
        src_new = jnp.concatenate(
            [jnp.where(core == 0, own_new, other_new), jnp.where(core == 0, other_new, own_new)]
        )
        tgt_new = epsilon * log_tgt - (epsilon * ln_2) * merge(parts) + tgt_potential
        return (src_new, tgt_new)

    placed = (
        P("row", None, None),
        P("col", None, None),
        P("row", None),
        P("col", None),
        P("col", None),
        P("row", None),
    )
    return jax.shard_map(
        on_device,
        mesh=mesh,
        in_specs=placed,
        out_specs=(P("row", None), P("col", None)),
        check_vma=False,
    )
```

```python
import functools
import math

import jax
import jax.numpy as jnp
from jax import lax
from jax.experimental import pallas as pl
from jax.experimental.pallas import tpu as pltpu
from jax.sharding import PartitionSpec as P

epsilon = 0.1
very_low = -1e30
tiny_sum = 2.0**-100
log2_e = math.log2(math.e)
ln_2 = math.log(2.0)
depth = 128
tail_rows = 16
unroll = 16
column_unroll = 8


def parts3(value):
    high = value.astype(jnp.bfloat16).astype(jnp.float32)
    rest = value - high
    middle = rest.astype(jnp.bfloat16).astype(jnp.float32)
    return high, middle, rest - middle


def merge(parts):
    top = parts[0]
    for part in parts[1:]:
        top = jnp.maximum(top, part)
    total = jnp.exp2(parts[0] - top)
    for part in parts[1:]:
        total = total + jnp.exp2(part - top)
    return top + jnp.log2(total)


def pad_rows(value, rows):
    return jnp.concatenate(
        [value, jnp.zeros((rows - value.shape[0],) + value.shape[1:], value.dtype)], axis=0
    )


def source_matrix(x_ref, s):
    x = x_ref[s]
    row = lax.broadcasted_iota(jnp.int32, (tail_rows, x.shape[1]), 0)
    ones = jnp.where(row < 3, 1.0, 0.0).astype(x.dtype)
    return pad_rows(jnp.concatenate([x, x, ones], axis=0), depth)


def bias_rows(value):
    high, middle, low = parts3(value)
    row = lax.broadcasted_iota(jnp.int32, (tail_rows, value.shape[-1]), 0)
    out = jnp.where(row == 0, high, jnp.where(row == 1, middle, jnp.where(row == 2, low, 0.0)))
    return out.astype(jnp.bfloat16)


def pair_product(s, t, x_ref, y_ref):
    return jnp.dot(y_ref[t], source_matrix(x_ref, s), preferred_element_type=jnp.float32)


def build_targets(points_ref, pot_ref, y_ref, offset):
    own, dim, cells = points_ref.shape
    scale = 2.0 * log2_e / (dim * epsilon)
    square_scale = log2_e / (dim * epsilon)

    def body(t, _):
        y = points_ref[t].astype(jnp.float32)
        bias = pot_ref[pl.ds(t, 1), :] * (log2_e / epsilon) - square_scale * jnp.sum(
            y * y, axis=0, keepdims=True
        )
        scaled = y * scale
        high = scaled.astype(jnp.bfloat16)
        low = (scaled - high.astype(jnp.float32)).astype(jnp.bfloat16)
        stacked = pad_rows(jnp.concatenate([high, low, bias_rows(bias)], axis=0), depth)
        y_ref[offset + t] = stacked.T
        return 0
    lax.fori_loop(0, own, body, 0, unroll=4)


def prepare_kernel(
    pattern_ref, points_ref, pot_ref, log_src_ref, src_ref,
    x_ref, square_ref, y_ref, log_ref, pot_out_ref, list_ref,
    pattern_scr, code_scr, code_smem, points_scr, sems,
):
    half, dim, cells = x_ref.shape
    own = points_ref.shape[0]
    pool = 2 * own
    fanout, sources = pattern_ref.shape
    square_scale = log2_e / (dim * epsilon)
    col = lax.axis_index("col")
    core = lax.rem(col, 2)
    base = (col - core) * own
    copies = [
        pltpu.make_async_copy(pattern_ref, pattern_scr, sems.at[0]),
        pltpu.make_async_copy(points_ref, points_scr, sems.at[1]),
        pltpu.make_async_copy(pot_ref, pot_out_ref, sems.at[2]),
        pltpu.make_async_copy(src_ref.at[pl.ds(core * half, half)], x_ref, sems.at[3]),
        pltpu.make_async_copy(log_src_ref.at[pl.ds(core * half, half)], log_ref, sems.at[5]),
    ]
    for copy in copies:
        copy.start()

    copies[0].wait()
    t = pattern_scr[...] - base
    inside = (t >= 0) & (t < pool)
    local = t + core * own
    local = jnp.where(local >= pool, local - pool, local)
    s = lax.broadcasted_iota(jnp.int32, (fanout, sources), 1) - core * half
    code_scr[...] = jnp.where(inside, (s << 10) | (local << 1) | 1, 0)
    code_copy = pltpu.make_async_copy(code_scr, code_smem, sems.at[4])
    code_copy.start()

    copies[1].wait()
    copies[2].wait()
    build_targets(points_scr, pot_out_ref, y_ref, 0)
    copies[3].wait()

    def build_square(s, _):
        x = x_ref[s].astype(jnp.float32)
        square_ref[pl.ds(s, 1), :] = jnp.sum(x * x, axis=0, keepdims=True) * square_scale
        return 0
    lax.fori_loop(0, half, build_square, 0, unroll=8)

    code_copy.wait()

    def scan(s, count):
        for k in range(fanout):
            code = code_smem[k, core * half + s]
            list_ref[count] = code >> 1
            count = count + (code & 1)
        return count
    end = lax.fori_loop(0, half, scan, jnp.int32(1), unroll=8)
    for k in range(unroll):
        list_ref[end + k] = jnp.int32(half << 20)
    list_ref[0] = end - 1
    copies[4].wait()


def pair_of(entry):
    return (entry >> 9) & 2047, entry & 511, entry >> 20


def row_kernel(
    list_ref, x_ref, square_ref, y_in_ref, other_ref, own_pot_ref, other_pot_ref,
    out_ref, shift_ref, y_ref, e_ref,
    z_ref, m_ref, s_used,
):
    half, dim, cells = x_ref.shape
    own = other_ref.shape[0]
    room = e_ref.shape[0]
    count = list_ref[0]
    turns = (count + unroll - 1) // unroll
    build_targets(other_ref, other_pot_ref, y_ref, own)
    top = jnp.maximum(jnp.max(own_pot_ref[...]), jnp.max(other_pot_ref[...])) * (
        log2_e / epsilon
    )
    z_ref[...] = jnp.zeros_like(z_ref)
    shift_ref[...] = -top - square_ref[...]

    def clear(s, _):
        s_used[s] = jnp.int32(0)
        return 0
    lax.fori_loop(0, half + 1, clear, 0)

    def scores(entry):
        s, t, pad = pair_of(entry)
        a = pair_product(s, t, x_ref, y_ref) + shift_ref[pl.ds(s, 1), :]
        return jnp.where(pad > 0, half, s), a

    def fast(turn, _):
        for k in range(unroll):
            at = turn * unroll + k
            row, a = scores(list_ref[1 + at])
            e = jnp.exp2(a)
            z_ref[row] += jnp.sum(e.reshape(cells // 8, 8, cells), axis=0)
            e_ref[jnp.minimum(at, room - 1)] = e.astype(jnp.bfloat16)
            s_used[row] = jnp.int32(1)
        return 0
    lax.fori_loop(0, turns, fast, 0)

    def finish(s, bad):
        total = jnp.sum(z_ref[s], axis=0, keepdims=True)
        used = s_used[s] > 0
        out_ref[pl.ds(s, 1), :] = jnp.where(used, top + jnp.log2(total), very_low)
        return jnp.maximum(bad, jnp.where((total < tiny_sum) & used, 1.0, 0.0))
    bad = lax.fori_loop(0, half, finish, jnp.zeros((1, cells), jnp.float32), unroll=8)

    @pl.when((jnp.max(bad) > 0.0) | (count > room))
    def _():
        def drop(at, _):
            e_ref[at] = jnp.zeros((cells, cells), jnp.bfloat16)
            return 0
        lax.fori_loop(0, room, drop, 0)
        z_ref[...] = jnp.zeros_like(z_ref)
        m_ref[...] = jnp.full_like(m_ref, very_low)

        def slow(turn, _):
            row, a = scores(list_ref[1 + turn])
            a = a.reshape(cells // 8, 8, cells)
            before = m_ref[row]
            after = jnp.maximum(before, jnp.max(a, axis=0))
            z_ref[row] = z_ref[row] * jnp.exp2(before - after) + jnp.sum(
                jnp.exp2(a - after[None]), axis=0
            )
            m_ref[row] = after
            return 0
        lax.fori_loop(0, count, slow, 0)

        def finish_slow(s, _):
            best = jnp.max(m_ref[s], axis=0, keepdims=True)
            total = jnp.sum(z_ref[s] * jnp.exp2(m_ref[s] - best), axis=0, keepdims=True)
            used = s_used[s] > 0
            out_ref[pl.ds(s, 1), :] = jnp.where(used, top + best + jnp.log2(total), very_low)
            return 0
        lax.fori_loop(0, half, finish_slow, 0)


def column_kernel(part_count, *refs):
    list_ref, x_ref, y_ref, e_ref, square_ref, row_shift_ref, log_ref = refs[:7]
    part_refs = refs[7 : 7 + part_count]
    own_ref, other_ref, new_ref = refs[7 + part_count : 10 + part_count]
    weight_ref, shift_ref, z_ref, m_ref, t_used = refs[10 + part_count :]
    half, dim, cells = x_ref.shape
    pool = y_ref.shape[0]
    own = pool // 2
    room = e_ref.shape[0]
    lanes = z_ref.shape[2]
    count = list_ref[0]
    turns = (count + column_unroll - 1) // column_unroll
    z_ref[...] = jnp.zeros_like(z_ref)
    for t in range(pool + 1):
        t_used[t] = jnp.int32(0)
    total = merge([ref[...] for ref in part_refs])
    mass = log_ref[...]
    new_ref[...] = epsilon * mass - (epsilon * ln_2) * total
    shift = mass * log2_e - square_ref[...] - total
    shift_ref[...] = shift
    weight = jnp.where(
        part_refs[0][...] > 0.5 * very_low, jnp.exp2(shift - row_shift_ref[...]), 0.0
    )
    weight_ref[...] = weight
    lowest = jnp.max(weight) * tiny_sum

    def row_of(entry):
        s, t, pad = pair_of(entry)
        return s, t, jnp.where(pad > 0, pool, t)

    def fast(turn, _):
        for k in range(column_unroll):
            at = turn * column_unroll + k
            s, t, slot = row_of(list_ref[1 + at])
            p = e_ref[jnp.minimum(at, room - 1)].astype(jnp.float32) * weight_ref[pl.ds(s, 1), :]
            z_ref[slot] += p[:, :lanes] + p[:, lanes:]
            t_used[slot] = jnp.int32(1)
        return 0
    lax.fori_loop(0, turns, fast, 0)

    ones = jnp.ones((16, lanes), jnp.bfloat16)

    def lane_sums(value):
        return lax.dot_general(
            ones, value, (((1,), (1,)), ((), ())), preferred_element_type=jnp.float32
        )[0:1]

    def finish(out_ref, offset):
        bad = jnp.zeros((1, cells), jnp.float32)
        for t in range(own):
            z = z_ref[offset + t]
            high = z.astype(jnp.bfloat16)
            low = (z - high.astype(jnp.float32)).astype(jnp.bfloat16)
            total = lane_sums(high) + lane_sums(low)
            used = t_used[offset + t] > 0
            out_ref[pl.ds(t, 1), :] = jnp.where(used, jnp.log2(total), very_low)
            bad = jnp.maximum(bad, jnp.where((total >= lowest) | ~used, 0.0, 1.0))
        return bad
    bad = jnp.maximum(finish(other_ref, own), finish(own_ref, 0))

    @pl.when(jnp.max(bad) > 0.0)
    def _():
        z_ref[...] = jnp.zeros_like(z_ref)
        m_ref[...] = jnp.full_like(m_ref, very_low)

        def slow(turn, _):
            s, t, slot = row_of(list_ref[1 + turn])
            a = pair_product(s, t, x_ref, y_ref) + shift_ref[pl.ds(s, 1), :]
            before = m_ref[slot]
            after = jnp.maximum(before, jnp.maximum(a[:, :lanes], a[:, lanes:]))
            z_ref[slot] = (
                z_ref[slot] * jnp.exp2(before - after)
                + jnp.exp2(a[:, :lanes] - after)
                + jnp.exp2(a[:, lanes:] - after)
            )
            m_ref[slot] = after
            t_used[slot] = jnp.int32(1)
            return 0
        lax.fori_loop(0, count, slow, 0)

        def finish_slow(out_ref, offset):
            def body(t, _):
                m = m_ref[offset + t]
                best = jnp.max(m, axis=1, keepdims=True)
                total = jnp.sum(z_ref[offset + t] * jnp.exp2(m - best), axis=1, keepdims=True)
                column = jnp.broadcast_to(best + jnp.log2(total), (cells, lanes))
                used = t_used[offset + t] > 0
                out_ref[pl.ds(t, 1), :] = jnp.where(used, column.T[0:1], very_low)
                return 0
            lax.fori_loop(0, own, body, 0)
        finish_slow(other_ref, own)
        finish_slow(own_ref, 0)


def needs(*shapes):
    return sum(math.prod(shape) * size for shape, size in shapes) + (4 << 20)


hbm = pl.BlockSpec(memory_space=pltpu.HBM)
smem = pl.BlockSpec(memory_space=pltpu.SMEM)
vmem = pl.BlockSpec(memory_space=pltpu.VMEM)


def prepare(pattern, points, potential, log_src, src_points):
    sources, dim, cells = src_points.shape
    half = sources // 2
    own = points.shape[0]
    fanout = pattern.shape[0]
    return pl.pallas_call(
        prepare_kernel,
        name="prepare",
        out_shape=(
            jax.ShapeDtypeStruct((half, dim, cells), src_points.dtype),
            jax.ShapeDtypeStruct((half, cells), jnp.float32),
            jax.ShapeDtypeStruct((2 * own, cells, depth), jnp.bfloat16),
            jax.ShapeDtypeStruct((half, cells), jnp.float32),
            jax.ShapeDtypeStruct((own, cells), jnp.float32),
            jax.ShapeDtypeStruct((half * fanout + unroll + 1,), jnp.int32),
        ),
        in_specs=[hbm] * 5,
        out_specs=(vmem, vmem, vmem, vmem, vmem, smem),
        scratch_shapes=[
            pltpu.VMEM(pattern.shape, jnp.int32),
            pltpu.VMEM(pattern.shape, jnp.int32),
            pltpu.SMEM(pattern.shape, jnp.int32),
            pltpu.VMEM(points.shape, points.dtype),
            pltpu.SemaphoreType.DMA((6,)),
        ],
        cost_estimate=pl.CostEstimate(
            flops=10 * src_points.size, bytes_accessed=2 * src_points.size, transcendentals=0
        ),
        compiler_params=pltpu.CompilerParams(
            vmem_limit_bytes=needs(
                ((half, dim, cells), 2), ((half, cells), 8), ((2 * own, cells, depth), 2),
                (points.shape, 2),
            )
        ),
    )(*[
        pltpu.with_memory_space_constraint(value, pltpu.HBM)
        for value in (pattern, points, potential, log_src, src_points)
    ])


def row_partials(pair_list, x, squares, targets, other, own_pot, other_pot, room):
    half, dim, cells = x.shape
    return pl.pallas_call(
        row_kernel,
        name="row_half_step",
        out_shape=(
            jax.ShapeDtypeStruct((half, cells), jnp.float32),
            jax.ShapeDtypeStruct((half, cells), jnp.float32),
            jax.ShapeDtypeStruct(targets.shape, targets.dtype),
            pltpu.VMEM((room, cells, cells), jnp.bfloat16),
        ),
        in_specs=[smem, vmem, vmem, vmem, vmem, vmem, vmem],
        out_specs=(vmem, vmem, vmem, vmem),
        input_output_aliases={3: 2},
        scratch_shapes=[
            pltpu.VMEM((half + 1, 8, cells), jnp.float32),
            pltpu.VMEM((half + 1, 8, cells), jnp.float32),
            pltpu.SMEM((half + 1,), jnp.int32),
        ],
        compiler_params=pltpu.CompilerParams(
            vmem_limit_bytes=needs(((half + 1, 8, cells), 8), ((half, cells), 8))
        ),
    )(pair_list, x, squares, targets, other, own_pot, other_pot)


def column_partials(pair_list, x, targets, kept, squares, shift, mass, parts):
    half, dim, cells = x.shape
    pool = targets.shape[0]
    lanes = cells // 2
    sums = jax.ShapeDtypeStruct((pool // 2, cells), jnp.float32)
    return pl.pallas_call(
        functools.partial(column_kernel, len(parts)),
        name="column_half_step",
        out_shape=(sums, sums, jax.ShapeDtypeStruct((half, cells), jnp.float32)),
        in_specs=[smem] + [vmem] * (6 + len(parts)),
        out_specs=(vmem, vmem, vmem),
        scratch_shapes=[
            pltpu.VMEM((half, cells), jnp.float32),
            pltpu.VMEM((half, cells), jnp.float32),
            pltpu.VMEM((pool + 1, cells, lanes), jnp.float32),
            pltpu.VMEM((pool + 1, cells, lanes), jnp.float32),
            pltpu.SMEM((pool + 1,), jnp.int32),
        ],
        compiler_params=pltpu.CompilerParams(
            vmem_limit_bytes=needs(((pool + 1, cells, lanes), 8), ((half, cells), 12))
        ),
    )(
        pair_list, x, targets, pltpu.with_memory_space_constraint(kept, pltpu.VMEM),
        squares, shift, mass, *parts
    )


def solution(mesh):
    def swap(value, axis, step):
        size = mesh.shape[axis]
        return lax.ppermute(value, axis, [(i, i ^ step) for i in range(size)])

    def rounds(axis, first):
        size = mesh.shape[axis]
        step = first
        while step < size:
            members = min(4, size // step)
            yield [k * step for k in range(1, members)]
            step *= members

    def on_device(src_points, tgt_points, log_src, log_tgt, tgt_potential, pattern):
        core = lax.rem(lax.axis_index("col"), 2)
        other_points = swap(tgt_points, "col", 1)
        other_potential = swap(tgt_potential, "col", 1)
        x, squares, targets, mass, own_potential, pair_list = prepare(
            pattern.T, tgt_points, tgt_potential, log_src, src_points
        )
        chips = mesh.shape["col"] // 2
        entries = x.shape[0] * pattern.shape[1]
        room = min(entries, 3 * -(-entries // (chips * unroll)) * unroll)
        left, shift, targets, kept = row_partials(
            pair_list, x, squares, targets, other_points, own_potential, other_potential, room
        )
        parts = [left]
        for strides in rounds("col", 2):
            left = merge(parts) if len(parts) > 1 else left
            parts = [left] + [swap(left, "col", stride) for stride in strides]
        own_sums, other_sums, own_new = column_partials(
            pair_list, x, targets, kept, squares, shift, mass, parts
        )
        parts = [own_sums, swap(other_sums, "col", 1)]
        other_new = swap(own_new, "col", 1)
        for strides in rounds("row", 1):
            total = merge(parts)
            parts = [total] + [swap(total, "row", stride) for stride in strides]
        src_new = jnp.concatenate(
            [jnp.where(core == 0, own_new, other_new), jnp.where(core == 0, other_new, own_new)]
        )
        tgt_new = epsilon * log_tgt - (epsilon * ln_2) * merge(parts) + tgt_potential
        return (src_new, tgt_new)

    placed = (
        P("row", None, None),
        P("col", None, None),
        P("row", None),
        P("col", None),
        P("col", None),
        P("row", None),
    )
    return jax.shard_map(
        on_device,
        mesh=mesh,
        in_specs=placed,
        out_specs=(P("row", None), P("col", None)),
        check_vma=False,
    )
```
